32 devices in a mesh: seq: 4 (over x, core), fsdp: 8 (over z, y).
Axes of the slice: x: 2, y: 2, z: 4, core: 2. Of those that a mesh axis runs over, the one named last changes fastest.
Arguments:
- hidden_in: bfloat16 [8, 1024, 2048], P('fsdp', 'seq'), may hold values from -6 to 6
- out_cotangent: bfloat16 [8, 1024, 2048], P('fsdp', 'seq'), may hold values from -6 to 6
- seg_ids: int32 [8, 1024], P('fsdp'), may hold values from 0 to 2, as said below
- mixer_master: float32 [2048, 2304], P(('seq', 'fsdp')), may hold values from -0.125 to 0.125
- mixer_first: float32 [2048, 2304], P(('seq', 'fsdp')), may hold values from -0.6 to 0.6
- mixer_second: float32 [2048, 2304], P(('seq', 'fsdp')), may hold values from 0.01 to 0.1
- project_master: float32 [2048, 2048], P(('seq', 'fsdp')), may hold values from -1 to 1
- project_first: float32 [2048, 2048], P(('seq', 'fsdp')), may hold values from -0.6 to 0.6
- project_second: float32 [2048, 2048], P(('seq', 'fsdp')), may hold values from 0.01 to 0.1
- expand_master: float32 [2048, 8192], P(('seq', 'fsdp')), may hold values from -0.125 to 0.125
- expand_first: float32 [2048, 8192], P(('seq', 'fsdp')), may hold values from -0.6 to 0.6
- expand_second: float32 [2048, 8192], P(('seq', 'fsdp')), may hold values from 0.01 to 0.1
- reduce_master: float32 [8192, 2048], P(('seq', 'fsdp')), may hold values from -0.0625 to 0.0625
- reduce_first: float32 [8192, 2048], P(('seq', 'fsdp')), may hold values from -0.6 to 0.6
- reduce_second: float32 [8192, 2048], P(('seq', 'fsdp')), may hold values from 0.01 to 0.1
- affine_master: float32 [4, 2048], replicated
- affine_first: float32 [4, 2048], replicated, may hold values from -0.6 to 0.6
- affine_second: float32 [4, 2048], replicated, may hold values from 0.1 to 20
Outputs:
- block_output: bfloat16 [8, 1024, 2048], P('fsdp', 'seq')
- input_grad: bfloat16 [8, 1024, 2048], P('fsdp', 'seq')
- grad_norm: float32 [], replicated
- mixer_updated: float32 [2048, 2304], P(('seq', 'fsdp'))
- mixer_first_new: float32 [2048, 2304], P(('seq', 'fsdp'))
- mixer_second_new: float32 [2048, 2304], P(('seq', 'fsdp'))
- project_updated: float32 [2048, 2048], P(('seq', 'fsdp'))
- project_first_new: float32 [2048, 2048], P(('seq', 'fsdp'))
- project_second_new: float32 [2048, 2048], P(('seq', 'fsdp'))
- expand_updated: float32 [2048, 8192], P(('seq', 'fsdp'))
- expand_first_new: float32 [2048, 8192], P(('seq', 'fsdp'))
- expand_second_new: float32 [2048, 8192], P(('seq', 'fsdp'))
- reduce_updated: float32 [8192, 2048], P(('seq', 'fsdp'))
- reduce_first_new: float32 [8192, 2048], P(('seq', 'fsdp'))
- reduce_second_new: float32 [8192, 2048], P(('seq', 'fsdp'))
- affine_step: float32 [4, 2048], replicated
- affine_first_new: float32 [4, 2048], replicated
- affine_second_new: float32 [4, 2048], replicated
The draws below stay inside these ranges and needn't reach their ends.
Inputs may be any that keep to these rules, and one draw needn't show every extreme that they name: `seg_ids`: in each group the prompt holds 512 tokens with id 0 and each of the 2 continuations (ids 1 to 2) holds 256 tokens; every segment is one contiguous run, in an order drawn for each group.
All inputs are finite; a program needn't handle non-finite values.
Results may differ from the reference program's by a relative error of at most 0.014.
Values may be sent and summed in bfloat16 or wider, within the bound.
No kernel may reach another device: no remote copies, remote signals or barrier semaphores. Data moves between devices by JAX's collectives and lax.ppermute only.
A program may use at most 576 MiB of HBM per device.

```python
import math
import jax
import jax.numpy as jnp
from jax import lax

D = 2048
FF = 8192
HEADS = 16
HEAD = 128
PROMPT = 512
NCONT = 2
CONT = 256
STEP = 10
GTOK = 1024
GROUPS = 8


def draw_seg_ids(key, part):

    def one_group(index):
        order = jax.random.permutation(jax.random.fold_in(key, index), NCONT + 1).astype(jnp.int32)
        lengths = jnp.where(order == 0, PROMPT, CONT).astype(jnp.int32)
        ends = jnp.cumsum(lengths).astype(jnp.int32)
        places = jnp.arange(GTOK, dtype=jnp.int32)
        which = jnp.sum((places[:, None] >= ends[None, :]).astype(jnp.int32), axis=1)
        return order[which]
    return jax.vmap(one_group)(jnp.arange(GROUPS, dtype=jnp.int32))


def draw_affine_master(key, part):
    noise = jax.random.normal(key, (4, D), jnp.float32)
    noise = jnp.clip(noise, -3.0, 3.0)
    row_index = jnp.arange(4, dtype=jnp.int32)[:, None]
    return jnp.where(row_index % 2 == 0, 1.0 + 0.15 * noise, 0.2 * noise)


def block_scale(own_key, extent, pieces, smallest, high):
    gain = 1.0
    for dim, parts in pieces:
        heights = jax.random.uniform(jax.random.fold_in(jax.random.fold_in(own_key, 6), dim), (parts,), jnp.float32, smallest / len(pieces), high / len(pieces))
        gain = gain * jnp.repeat(jnp.exp(heights), extent[dim] // parts).reshape((-1,) + (1,) * (len(extent) - 1 - dim))
    return gain


def bell_draw(own_key, extent, scale, reach, shards=(), kind=jnp.bfloat16):
    drawn = scale * jax.random.normal(own_key, extent, jnp.float32)
    if shards:
        drawn = drawn * block_scale(own_key, extent, shards, -0.22, 0.18)
    return jnp.clip(drawn, -reach, reach).astype(kind)


def setup_inputs(seed: int = 0) -> dict:
    streams_of = jax.random.split(jax.random.key(seed), 19)
    hidden_in = bell_draw(streams_of[0], (GROUPS, GTOK, D), 1.0, 6.0, ((0, 8), (1, 4)))
    out_cotangent = bell_draw(streams_of[1], (GROUPS, GTOK, D), 1.0, 6.0, ((0, 8), (1, 4)))
    seg_ids = draw_seg_ids(jax.random.fold_in(streams_of[18], 71), 0)
    mixer_master = bell_draw(streams_of[3], (D, D + 2 * HEAD), D ** -0.5, 0.125, ((0, 32),), jnp.float32)
    mixer_first = bell_draw(streams_of[4], (D, D + 2 * HEAD), 0.1, 0.6, ((0, 32),), jnp.float32)
    mixer_second = jnp.clip(jnp.exp(math.log(0.1) - 2.3025851 * jax.random.uniform(streams_of[5], (D, D + 2 * HEAD), jnp.float32) ** block_scale(streams_of[5], (D, D + 2 * HEAD), ((0, 32),), -0.2, 0.2)), 0.01, 0.1)
    project_master = bell_draw(streams_of[6], (D, D), (D // 64) ** -0.5, 1.0, ((0, 32),), jnp.float32)
    project_first = bell_draw(streams_of[7], (D, D), 0.1, 0.6, ((0, 32),), jnp.float32)
    project_second = jnp.clip(jnp.exp(math.log(0.1) - 2.3025851 * jax.random.uniform(streams_of[8], (D, D), jnp.float32) ** block_scale(streams_of[8], (D, D), ((0, 32),), -0.2, 0.2)), 0.01, 0.1)
    expand_master = bell_draw(streams_of[9], (D, FF), D ** -0.5, 0.125, ((0, 32),), jnp.float32)
    expand_first = bell_draw(streams_of[10], (D, FF), 0.1, 0.6, ((0, 32),), jnp.float32)
    expand_second = jnp.clip(jnp.exp(math.log(0.1) - 2.3025851 * jax.random.uniform(streams_of[11], (D, FF), jnp.float32) ** block_scale(streams_of[11], (D, FF), ((0, 32),), -0.2, 0.2)), 0.01, 0.1)
    reduce_master = bell_draw(streams_of[12], (FF, D), FF ** -0.5, 0.0625, ((0, 32),), jnp.float32)
    reduce_first = bell_draw(streams_of[13], (FF, D), 0.1, 0.6, ((0, 32),), jnp.float32)
    reduce_second = jnp.clip(jnp.exp(math.log(0.1) - 2.3025851 * jax.random.uniform(streams_of[14], (FF, D), jnp.float32) ** block_scale(streams_of[14], (FF, D), ((0, 32),), -0.2, 0.2)), 0.01, 0.1)
    affine_master = draw_affine_master(jax.random.fold_in(streams_of[18], 71), 0)
    affine_first = bell_draw(streams_of[16], (4, D), 0.1, 0.6, (), jnp.float32)
    affine_second = jnp.clip(jnp.exp(jax.random.uniform(streams_of[17], (4, D), jnp.float32, math.log(0.1), math.log(20.0))), 0.1, 20.0)
    return dict(hidden_in=hidden_in, out_cotangent=out_cotangent, seg_ids=seg_ids, mixer_master=mixer_master, mixer_first=mixer_first, mixer_second=mixer_second, project_master=project_master, project_first=project_first, project_second=project_second, expand_master=expand_master, expand_first=expand_first, expand_second=expand_second, reduce_master=reduce_master, reduce_first=reduce_first, reduce_second=reduce_second, affine_master=affine_master, affine_first=affine_first, affine_second=affine_second)


@jax.custom_vjp
def low(v):
    return lax.optimization_barrier(v.astype(jnp.bfloat16)).astype(jnp.float32)

@jax.custom_vjp
def low_back(v):
    return v

def low_keep(v):
    return (low(v), None)

def low_pass(kept, grad):
    return (grad,)

def back_keep(v):
    return (v, None)

def back_low(kept, grad):
    return (low(grad),)
low.defvjp(low_keep, low_pass)
low_back.defvjp(back_keep, back_low)
highest = lax.Precision.HIGHEST
norm_epsilon = 1e-05
adam_epsilon = 1e-08
first_decay = 0.9
second_decay = 0.95
learn_rate = 0.03
decay_rate = 0.1
masked_score = -1e+30

def layer_norm(values_in, norm_gain, norm_shift):
    centered = values_in - lax.optimization_barrier(jnp.mean(values_in, axis=-1, keepdims=True))
    variance = lax.optimization_barrier(jnp.mean(centered * centered, axis=-1, keepdims=True))
    return centered * lax.rsqrt(variance + norm_epsilon) * norm_gain + norm_shift

def activate(pre_act):
    return jax.nn.gelu(pre_act, approximate=True)

def product(left_side, right_side):
    return jnp.dot(left_side, right_side, precision=highest, preferred_element_type=jnp.float32)

def visible(query_place, query_segment, segments):
    key_place = jnp.arange(segments.shape[0], dtype=jnp.int32)
    same_segment = (segments[None, :] == query_segment[:, None]) & (key_place[None, :] <= query_place[:, None])
    prompt_shared = (segments[None, :] == 0) & (query_segment[:, None] != 0)
    return same_segment | prompt_shared

def attend(queries, key_rows, value_rows, segments):
    block_size = math.gcd(GTOK, 512)
    places = jnp.arange(GTOK, dtype=jnp.int32)
    scale = HEAD ** (-0.5)

    def one_block(row_start):
        query_rows = lax.dynamic_slice_in_dim(queries, row_start, block_size, 0)
        allowed = visible(lax.dynamic_slice_in_dim(places, row_start, block_size, 0), lax.dynamic_slice_in_dim(segments, row_start, block_size, 0), segments)
        scores = jnp.einsum('qhd,kd->hqk', query_rows, key_rows, precision=highest) * scale
        scores = jnp.where(allowed[None], low_back(scores), masked_score)
        top_score = lax.optimization_barrier(jnp.max(scores, axis=-1, keepdims=True))
        exp_scores = jnp.exp(scores - top_score)
        probs = low(exp_scores / lax.optimization_barrier(jnp.sum(exp_scores, axis=-1, keepdims=True)))
        mixed_out = jnp.einsum('hqk,kd->qhd', probs, value_rows, precision=highest)
        return low(low_back(mixed_out))
    block_starts = jnp.arange(0, GTOK, block_size, dtype=jnp.int32)
    return lax.map(jax.checkpoint(one_block), block_starts).reshape(GTOK, HEADS * HEAD)

def group_forward(hidden, segments, mixer_w, project_w, expand_w, reduce_w, affine):
    ln_one = low(layer_norm(hidden, affine[0], affine[1]))
    mixed = low(low_back(product(ln_one, mixer_w)))
    queries = mixed[:, :D].reshape(GTOK, HEADS, HEAD)
    attended = attend(queries, mixed[:, D:D + HEAD], mixed[:, D + HEAD:], segments)
    middle = hidden + low_back(product(attended, project_w))
    ln_two = low(layer_norm(middle, affine[2], affine[3]))
    expanded = low_back(product(ln_two, expand_w))
    return middle + product(low(activate(expanded)), reduce_w)

def adam_update(master, first, second, gradient, factor):
    clipped = gradient * factor
    first_new = first_decay * first + (1.0 - first_decay) * clipped
    second_new = second_decay * second + (1.0 - second_decay) * clipped * clipped
    first_hat = first_new / (1.0 - first_decay ** STEP)
    second_hat = second_new / (1.0 - second_decay ** STEP)
    updated = master - learn_rate * (first_hat / (jnp.sqrt(second_hat) + adam_epsilon) + decay_rate * master)
    return (updated, first_new, second_new)

def reference(hidden_in, out_cotangent, seg_ids, mixer_master, mixer_first, mixer_second, project_master, project_first, project_second, expand_master, expand_first, expand_second, reduce_master, reduce_first, reduce_second, affine_master, affine_first, affine_second):

    def forward(hidden, mixer_w, project_w, expand_w, reduce_w, affine):

        def one_group(pair):
            return group_forward(pair[0], pair[1], mixer_w, project_w, expand_w, reduce_w, affine)
        return lax.map(jax.checkpoint(one_group), (hidden, seg_ids))
    output, pullback = jax.vjp(forward, hidden_in.astype(jnp.float32), low(mixer_master), low(project_master), low(expand_master), low(reduce_master), affine_master)
    grads = pullback(out_cotangent.astype(jnp.float32))
    mixer_grad, project_grad, expand_grad, reduce_grad, affine_grad = (grads[1], grads[2], grads[3], grads[4], grads[5])
    square_total = jnp.sum(mixer_grad * mixer_grad) + jnp.sum(project_grad * project_grad) + jnp.sum(expand_grad * expand_grad) + jnp.sum(reduce_grad * reduce_grad) + jnp.sum(affine_grad * affine_grad)
    grad_norm = jnp.sqrt(square_total)
    limit = math.sqrt(float(D * (D + 2 * HEAD) + D * D + 2 * D * FF + 4 * D))
    factor = limit / jnp.maximum(grad_norm, limit)
    mixer_state = adam_update(mixer_master, mixer_first, mixer_second, mixer_grad, factor)
    project_state = adam_update(project_master, project_first, project_second, project_grad, factor)
    expand_state = adam_update(expand_master, expand_first, expand_second, expand_grad, factor)
    reduce_state = adam_update(reduce_master, reduce_first, reduce_second, reduce_grad, factor)
    affine_state = adam_update(affine_master, affine_first, affine_second, affine_grad, factor)
    return (output.astype(jnp.bfloat16), grads[0].astype(jnp.bfloat16), grad_norm, mixer_state[0], mixer_state[1], mixer_state[2], project_state[0], project_state[1], project_state[2], expand_state[0], expand_state[1], expand_state[2], reduce_state[0], reduce_state[1], reduce_state[2], affine_state[0] - affine_master, affine_state[1], affine_state[2])
```

```python
import math

import jax
import jax.numpy as jnp
from jax import lax
from jax.sharding import PartitionSpec as P

D = 2048
FF = 8192
HEADS = 16
HEAD = 128
STEP = 10
KV = 2 * HEAD

norm_epsilon = 1e-05
adam_epsilon = 1e-08
first_decay = 0.9
second_decay = 0.95
learn_rate = 0.03
decay_rate = 0.1
masked_score = -1e30
low = jnp.bfloat16


def layer_norm(values_in, norm_gain, norm_shift):
    centered = values_in - jnp.mean(values_in, axis=-1, keepdims=True)
    variance = jnp.mean(centered * centered, axis=-1, keepdims=True)
    return centered * lax.rsqrt(variance + norm_epsilon) * norm_gain + norm_shift


def activate(pre_act):
    return jax.nn.gelu(pre_act, approximate=True)


def product(left_side, right_side):
    return jnp.dot(left_side, right_side, preferred_element_type=jnp.float32)


def times_transpose(left_side, right_side):
    return lax.dot_general(
        left_side, right_side, (((1,), (1,)), ((), ())), preferred_element_type=jnp.float32
    )


def column_product(left_side, right_side):
    return lax.dot_general(
        left_side, right_side, (((0,), (0,)), ((), ())), preferred_element_type=jnp.float32
    )


def swap(value, axis, count, distance):
    return lax.ppermute(value, axis, [(i, i ^ distance) for i in range(count)])


def gather_tokens(own, count):
    blocks = {0: own}
    distance = count // 2
    while distance:
        held = sorted(blocks)
        packed = jnp.concatenate([blocks[k] for k in held]) if len(held) > 1 else own
        come = swap(packed, "seq", count, distance)
        rows = own.shape[0]
        for place, k in enumerate(held):
            blocks[k ^ distance] = come[place * rows : (place + 1) * rows]
        distance //= 2
    return jnp.concatenate([blocks[k] for k in range(count)])


def scatter_tokens(partial, count):
    rows = partial.shape[0] // count
    blocks = {k: partial[k * rows : (k + 1) * rows] for k in range(count)}
    distance = 1
    while distance < count:
        leave = sorted(k for k in blocks if k & distance)
        packed = jnp.concatenate([blocks[k].astype(low) for k in leave])
        come = swap(packed, "seq", count, distance)
        for place, k in enumerate(leave):
            got = come[place * rows : (place + 1) * rows].astype(jnp.float32)
            blocks[k ^ distance] = blocks[k ^ distance] + got
            del blocks[k]
        distance *= 2
    return blocks[0]


def exchange(block_of, member, count):
    first = block_of(member)
    result = jnp.zeros((count,) + first.shape, first.dtype)
    result = lax.dynamic_update_slice_in_dim(result, first[None], member, 0)
    for k in range(1, count):
        come = swap(block_of(member ^ k), "seq", count, k)
        result = lax.dynamic_update_slice_in_dim(result, come[None], member ^ k, 0)
    return result


def visible(query_place, query_segment, places, segments):
    same_segment = (segments[None, :] == query_segment[:, None]) & (
        places[None, :] <= query_place[:, None]
    )
    prompt_shared = (segments[None, :] == 0) & (query_segment[:, None] != 0)
    return same_segment | prompt_shared


def block_scores(queries, key_rows, places, segments, row_start, block_size):
    query_rows = lax.dynamic_slice_in_dim(queries, row_start, block_size, 0)
    allowed = visible(
        lax.dynamic_slice_in_dim(places, row_start, block_size, 0),
        lax.dynamic_slice_in_dim(segments, row_start, block_size, 0),
        places,
        segments,
    )
    scores = jnp.einsum(
        "qhd,kd->hqk", query_rows, key_rows, preferred_element_type=jnp.float32
    ) * queries.shape[2] ** (-0.5)
    return (query_rows, jnp.where(allowed[None], scores, masked_score))


def attend_forward(queries, key_rows, value_rows, places, segments):
    row_total = queries.shape[0]
    block_size = math.gcd(row_total, 512)

    def one_block(row_start):
        query_rows, scores = block_scores(
            queries, key_rows, places, segments, row_start, block_size
        )
        top_score = jnp.max(scores, axis=-1, keepdims=True)
        exp_scores = jnp.exp(scores - top_score)
        exp_total = jnp.sum(exp_scores, axis=-1, keepdims=True)
        probs_low = (exp_scores / exp_total).astype(low)
        mixed_out = jnp.einsum(
            "hqk,kd->qhd", probs_low, value_rows, preferred_element_type=jnp.float32
        )
        return (mixed_out.astype(low), (top_score + jnp.log(exp_total))[:, :, 0])

    block_starts = jnp.arange(0, row_total, block_size, dtype=jnp.int32)
    block_outs, logsum = lax.map(one_block, block_starts)
    return (block_outs.reshape(queries.shape), logsum)


def attend_backward(queries, key_rows, value_rows, logsum, grad_out, places, segments):
    row_total = queries.shape[0]
    block_size = math.gcd(row_total, 512)
    scale = queries.shape[2] ** (-0.5)

    def one_block(carry_in, block_item):
        row_start, block_logsum = block_item
        query_rows, scores = block_scores(
            queries, key_rows, places, segments, row_start, block_size
        )
        probs = jnp.exp(scores - block_logsum[:, :, None])
        grad_rows = lax.dynamic_slice_in_dim(grad_out, row_start, block_size, 0)
        grad_probs = jnp.einsum(
            "qhd,kd->hqk", grad_rows, value_rows, preferred_element_type=jnp.float32
        )
        inner_sum = jnp.sum(probs * grad_probs, axis=-1, keepdims=True)
        grad_scores = (probs * (grad_probs - inner_sum)).astype(low)
        query_grad = (
            jnp.einsum("hqk,kd->qhd", grad_scores, key_rows, preferred_element_type=jnp.float32)
            * scale
        )
        key_grad = (
            carry_in[0]
            + jnp.einsum("hqk,qhd->kd", grad_scores, query_rows, preferred_element_type=jnp.float32)
            * scale
        )
        value_grad = carry_in[1] + jnp.einsum(
            "hqk,qhd->kd", probs.astype(low), grad_rows, preferred_element_type=jnp.float32
        )
        return ((key_grad, value_grad), query_grad.astype(low))

    block_starts = jnp.arange(0, row_total, block_size, dtype=jnp.int32)
    zero_grad = jnp.zeros(key_rows.shape, jnp.float32)
    (key_grad, value_grad), query_grads = lax.scan(
        one_block, (zero_grad, zero_grad), (block_starts, logsum)
    )
    return (query_grads.reshape(queries.shape), jnp.concatenate([key_grad, value_grad], axis=1))


def adam_update(master, first, second, gradient, factor):
    clipped = gradient * factor
    first_new = first_decay * first + (1.0 - first_decay) * clipped
    second_new = second_decay * second + (1.0 - second_decay) * clipped * clipped
    first_hat = first_new / (1.0 - first_decay**STEP)
    second_hat = second_new / (1.0 - second_decay**STEP)
    updated = master - learn_rate * (
        first_hat / (jnp.sqrt(second_hat) + adam_epsilon) + decay_rate * master
    )
    return (updated, first_new, second_new)


def gather_weight(value, dim):
    return lax.all_gather(value, "fsdp", axis=dim, tiled=True)


def scatter_grad(value, dim):
    return lax.psum_scatter(
        value.astype(low), "fsdp", scatter_dimension=dim, tiled=True
    ).astype(jnp.float32)


def local_step(
    count,
    hidden_in,
    out_cotangent,
    seg_ids,
    mixer_master,
    mixer_first,
    mixer_second,
    project_master,
    project_first,
    project_second,
    expand_master,
    expand_first,
    expand_second,
    reduce_master,
    reduce_first,
    reduce_second,
    affine_master,
    affine_first,
    affine_second,
):
    member = lax.axis_index("seq")
    token_count = hidden_in.shape[1]
    group_tokens = token_count * count
    heads = HEADS // count
    width = heads * HEAD
    slab = FF // count
    hidden = hidden_in[0].astype(jnp.float32)
    segment_rows = seg_ids[0].reshape(count, token_count)
    owners = [member ^ k for k in range(count)]
    segments = jnp.concatenate([segment_rows[m] for m in owners])
    places = jnp.concatenate(
        [m * token_count + jnp.arange(token_count, dtype=jnp.int32) for m in owners]
    )

    mixer_low = mixer_master.astype(low)
    expand_low = expand_master.astype(low)

    def mixer_block(m):
        return jnp.concatenate(
            [lax.dynamic_slice_in_dim(mixer_low, m * width, width, 1), mixer_low[:, D:]], axis=1
        )

    def expand_block(m):
        return lax.dynamic_slice_in_dim(expand_low, m * slab, slab, 1)

    mixer_w = gather_weight(exchange(mixer_block, member, count), 1).reshape(D, width + KV)
    project_w = gather_weight(project_master.astype(low), 0)
    expand_w = gather_weight(exchange(expand_block, member, count), 1).reshape(D, slab)
    reduce_w = gather_weight(reduce_master.astype(low), 0)

    ln_one = gather_tokens(
        layer_norm(hidden, affine_master[0], affine_master[1]).astype(low), count
    )
    mixed = product(ln_one, mixer_w).astype(low)
    queries = mixed[:, :width].reshape(group_tokens, heads, HEAD)
    key_rows = mixed[:, width : width + HEAD]
    value_rows = mixed[:, width + HEAD :]
    head_out, logsum = attend_forward(queries, key_rows, value_rows, places, segments)
    attended = head_out.reshape(group_tokens, width)
    middle = hidden + scatter_tokens(product(attended, project_w), count)
    ln_two = gather_tokens(
        layer_norm(middle, affine_master[2], affine_master[3]).astype(low), count
    )
    cotangent = gather_tokens(out_cotangent[0], count)
    expanded = product(ln_two, expand_w)
    activated = activate(expanded).astype(low)
    output = middle + scatter_tokens(product(activated, reduce_w), count)
    block_output = output.astype(low)[None]

    reduce_grad = scatter_grad(column_product(activated, cotangent), 0)
    grad_activated = times_transpose(cotangent, reduce_w)
    gelu_value, gelu_pull = jax.vjp(activate, expanded)
    grad_expanded = gelu_pull(grad_activated)[0].astype(low)
    grad_normed = scatter_tokens(times_transpose(grad_expanded, expand_w), count)
    expand_part = scatter_grad(
        column_product(ln_two, grad_expanded).reshape(count, D // count, slab), 1
    )
    expand_grad = exchange(lambda m: expand_part[m], member, count)
    expand_grad = jnp.moveaxis(expand_grad, 0, 1).reshape(expand_master.shape)
    second_value, second_pull = jax.vjp(layer_norm, middle, affine_master[2], affine_master[3])
    grad_inner, gain_two, shift_two = second_pull(grad_normed)
    grad_middle = out_cotangent[0].astype(jnp.float32) + grad_inner
    grad_branch = gather_tokens(grad_middle.astype(low), count)
    grad_head = (
        times_transpose(grad_branch, project_w).astype(low).reshape(group_tokens, heads, HEAD)
    )
    query_part, key_value_part = attend_backward(
        queries, key_rows, value_rows, logsum, grad_head, places, segments
    )
    project_grad = scatter_grad(column_product(attended, grad_branch), 0)
    grad_mixed = jnp.concatenate(
        [query_part.reshape(group_tokens, width), key_value_part.astype(low)], axis=1
    )
    mixer_part = scatter_grad(
        column_product(ln_one, grad_mixed).reshape(count, D // count, width + KV), 1
    )
    mixer_part = exchange(lambda m: mixer_part[m], member, count)
    mixer_grad = jnp.concatenate(
        [
            jnp.moveaxis(mixer_part[:, :, :width], 0, 1).reshape(-1, D),
            jnp.sum(mixer_part[:, :, width:], axis=0),
        ],
        axis=1,
    )
    grad_first = scatter_tokens(times_transpose(grad_mixed, mixer_w), count)
    first_value, first_pull = jax.vjp(layer_norm, hidden, affine_master[0], affine_master[1])
    grad_hidden, gain_one, shift_one = first_pull(grad_first)
    input_grad = (grad_middle + grad_hidden).astype(low)[None]

    affine_grad = lax.psum(jnp.stack([gain_one, shift_one, gain_two, shift_two]), ("seq", "fsdp"))
    local_square = (
        jnp.sum(mixer_grad * mixer_grad)
        + jnp.sum(project_grad * project_grad)
        + jnp.sum(expand_grad * expand_grad)
        + jnp.sum(reduce_grad * reduce_grad)
    )
    square_total = lax.psum(local_square, ("seq", "fsdp")) + jnp.sum(affine_grad * affine_grad)
    grad_norm = jnp.sqrt(square_total)
    limit = math.sqrt(float(D * (D + KV) + D * D + 2 * D * FF + 4 * D))
    factor = limit / jnp.maximum(grad_norm, limit)
    mixer_state = adam_update(mixer_master, mixer_first, mixer_second, mixer_grad, factor)
    project_state = adam_update(project_master, project_first, project_second, project_grad, factor)
    expand_state = adam_update(expand_master, expand_first, expand_second, expand_grad, factor)
    reduce_state = adam_update(reduce_master, reduce_first, reduce_second, reduce_grad, factor)
    affine_state = adam_update(affine_master, affine_first, affine_second, affine_grad, factor)
    return (
        block_output,
        input_grad,
        grad_norm,
        *mixer_state,
        *project_state,
        *expand_state,
        *reduce_state,
        affine_state[0] - affine_master,
        affine_state[1],
        affine_state[2],
    )


def solution(mesh):
    count = mesh.shape["seq"]
    tokens = P("fsdp", "seq", None)
    rows = P(("seq", "fsdp"), None)
    in_specs = (tokens, tokens, P("fsdp", None)) + (rows,) * 12 + (P(),) * 3
    out_specs = (tokens, tokens, P()) + (rows,) * 12 + (P(),) * 3

    def local(*values):
        return local_step(count, *values)

    return jax.shard_map(local, mesh=mesh, in_specs=in_specs, out_specs=out_specs, check_vma=False)
```

```python
import functools
import math

import jax
import jax.numpy as jnp
from jax import lax
from jax.experimental import pallas as pl
from jax.experimental.pallas import tpu as pltpu
from jax.sharding import PartitionSpec as P


D = 2048
FF = 8192
HEADS = 16
HEAD = 128
STEP = 10
KV = 2 * HEAD

norm_epsilon = 1e-05
adam_epsilon = 1e-08
first_decay = 0.9
second_decay = 0.95
learn_rate = 0.03
decay_rate = 0.1
masked_score = -1e30
low = jnp.bfloat16


def layer_norm(values_in, norm_gain, norm_shift):
    centered = values_in - jnp.mean(values_in, axis=-1, keepdims=True)
    variance = jnp.mean(centered * centered, axis=-1, keepdims=True)
    return centered * lax.rsqrt(variance + norm_epsilon) * norm_gain + norm_shift


def activate(pre_act):
    return jax.nn.gelu(pre_act, approximate=True)


def product(left_side, right_side):
    return jnp.dot(left_side, right_side, preferred_element_type=jnp.float32)


def times_transpose(left_side, right_side):
    return lax.dot_general(
        left_side, right_side, (((1,), (1,)), ((), ())), preferred_element_type=jnp.float32
    )


def column_product(left_side, right_side):
    return lax.dot_general(
        left_side, right_side, (((0,), (0,)), ((), ())), preferred_element_type=jnp.float32
    )


def swap(value, axis, count, distance):
    return lax.ppermute(value, axis, [(i, i ^ distance) for i in range(count)])


def gather_tokens(own, count):
    held = own
    distance = count // 2
    while distance:
        held = jnp.concatenate([held, swap(held, "seq", count, distance)])
        distance //= 2
    return held


def scatter_tokens(make, rows, count):
    held = None
    distance = 1
    while distance < count:
        part = rows // 2
        if held is None:
            leave = make(part, rows).astype(low)
            stay = make(0, part)
        else:
            leave = held[part:].astype(low)
            stay = held[:part]
        held = stay + swap(leave, "seq", count, distance).astype(jnp.float32)
        rows = part
        distance *= 2
    return held


def gather_rows(own, member, count, filler):
    blocks = {0: own}
    distance = count // 2
    while distance:
        for k in sorted(blocks):
            blocks[k ^ distance] = swap(blocks[k], "fsdp", count, distance)
        distance //= 2
    lead, rows, columns = own.shape
    result = jnp.broadcast_to(filler, (lead, count, rows, columns))
    for k in range(count):
        result = lax.dynamic_update_slice_in_dim(result, blocks[k][:, None], member ^ k, 1)
    return result.reshape(lead * count * rows, columns)


def scatter_step(value, member, count, remaining, distance):
    lead, rows, columns = value.shape
    above = 2 ** sum(d > distance for d in remaining)
    pairs = value.reshape(lead, above, 2, rows // (2 * above), columns)
    bit = (member // distance) % 2
    leave = lax.dynamic_index_in_dim(pairs, 1 - bit, 2, keepdims=False)
    come = swap(leave.astype(low), "fsdp", count, distance)
    kept = lax.dynamic_index_in_dim(pairs, bit, 2, keepdims=False) + come.astype(jnp.float32)
    return kept.reshape(lead, rows // 2, columns)


def scatter_rows(value, member, count):
    remaining = [2**k for k in range(count.bit_length() - 1)]
    for distance in list(remaining):
        value = scatter_step(value, member, count, remaining, distance)
        remaining = [d for d in remaining if d != distance]
    return value


def scatter_mixed(value, member, count):
    remaining = [2**k for k in range(count.bit_length() - 1)]
    kept = scatter_step(value, member, count, remaining, 1)
    kept = kept.astype(low)
    groups = [[y + 2 * z for z in range(count // 2)] for y in range(2)]
    return lax.psum_scatter(kept, "fsdp", scatter_dimension=1, tiled=True, axis_index_groups=groups)


def total_over_mesh(value, place, counts):
    spots = jnp.arange(8 * 128, dtype=jnp.int32).reshape(8, 128)
    spread = jnp.where(spots == place, value, 0.0)
    for axis, count in counts:
        come = [swap(spread, axis, count, k) for k in range(1, count)]
        for part in come:
            spread = spread + part
    return jnp.sum(spread)


def butterfly(value, counts):
    for axis, count in counts:
        distance = 1
        while distance < count:
            value = value + swap(value, axis, count, distance)
            distance *= 2
    return value


def trade(block_of, member, count):
    return [block_of(member)] + [
        swap(block_of(member ^ k), "seq", count, k) for k in range(1, count)
    ]


def exchange(block_of, member, count):
    pieces = trade(block_of, member, count)
    result = jnp.broadcast_to(pieces[0], (count,) + pieces[0].shape)
    for k, piece in enumerate(pieces):
        result = lax.dynamic_update_slice_in_dim(result, piece[None], member ^ k, 0)
    return lax.optimization_barrier(result)


def visible(query_place, query_segment, places, segments):
    same_segment = (segments[None, :] == query_segment[:, None]) & (
        places[None, :] <= query_place[:, None]
    )
    prompt_shared = (segments[None, :] == 0) & (query_segment[:, None] != 0)
    return same_segment | prompt_shared


def block_scores(queries, key_rows, places, segments, row_start, block_size):
    query_rows = lax.dynamic_slice_in_dim(queries, row_start, block_size, 0)
    allowed = visible(
        lax.dynamic_slice_in_dim(places, row_start, block_size, 0),
        lax.dynamic_slice_in_dim(segments, row_start, block_size, 0),
        places,
        segments,
    )
    scores = jnp.einsum(
        "qhd,kd->hqk", query_rows, key_rows, preferred_element_type=jnp.float32
    ) * queries.shape[2] ** (-0.5)
    return (query_rows, jnp.where(allowed[None], scores, masked_score))


def attend_forward(queries, key_rows, value_rows, places, segments):
    row_total = queries.shape[0]
    block_size = math.gcd(row_total, 512)

    def one_block(row_start):
        _, scores = block_scores(queries, key_rows, places, segments, row_start, block_size)
        top_score = jnp.max(scores, axis=-1, keepdims=True)
        exp_scores = jnp.exp(scores - top_score)
        exp_total = jnp.sum(exp_scores, axis=-1, keepdims=True)
        probs_low = (exp_scores / exp_total).astype(low)
        mixed_out = jnp.einsum(
            "hqk,kd->qhd", probs_low, value_rows, preferred_element_type=jnp.float32
        )
        return (mixed_out.astype(low), (top_score + jnp.log(exp_total))[:, :, 0])

    block_starts = jnp.arange(0, row_total, block_size, dtype=jnp.int32)
    block_outs, logsum = lax.map(one_block, block_starts)
    return (block_outs.reshape(queries.shape), logsum)


def attend_backward(queries, key_rows, value_rows, logsum, grad_out, places, segments):
    row_total = queries.shape[0]
    block_size = math.gcd(row_total, 512)
    scale = queries.shape[2] ** (-0.5)

    def one_block(carry_in, block_item):
        row_start, block_logsum = block_item
        query_rows, scores = block_scores(
            queries, key_rows, places, segments, row_start, block_size
        )
        probs = jnp.exp(scores - block_logsum[:, :, None])
        grad_rows = lax.dynamic_slice_in_dim(grad_out, row_start, block_size, 0)
        grad_probs = jnp.einsum(
            "qhd,kd->hqk", grad_rows, value_rows, preferred_element_type=jnp.float32
        )
        inner_sum = jnp.sum(probs * grad_probs, axis=-1, keepdims=True)
        grad_scores = (probs * (grad_probs - inner_sum)).astype(low)
        query_grad = (
            jnp.einsum("hqk,kd->qhd", grad_scores, key_rows, preferred_element_type=jnp.float32)
            * scale
        )
        key_grad = (
            carry_in[0]
            + jnp.einsum("hqk,qhd->kd", grad_scores, query_rows, preferred_element_type=jnp.float32)
            * scale
        )
        value_grad = carry_in[1] + jnp.einsum(
            "hqk,qhd->kd", probs.astype(low), grad_rows, preferred_element_type=jnp.float32
        )
        return ((key_grad, value_grad), query_grad.astype(low))

    block_starts = jnp.arange(0, row_total, block_size, dtype=jnp.int32)
    zero_grad = jnp.zeros(key_rows.shape, jnp.float32)
    (key_grad, value_grad), query_grads = lax.scan(
        one_block, (zero_grad, zero_grad), (block_starts, logsum)
    )
    return (query_grads.reshape(queries.shape), jnp.concatenate([key_grad, value_grad], axis=1))


def adam_update(master, first, second, gradient, factor):
    clipped = gradient * factor
    first_new = first_decay * first + (1.0 - first_decay) * clipped
    second_new = second_decay * second + (1.0 - second_decay) * clipped * clipped
    first_hat = first_new / (1.0 - first_decay**STEP)
    second_hat = second_new / (1.0 - second_decay**STEP)
    updated = master - learn_rate * (
        first_hat / (jnp.sqrt(second_hat) + adam_epsilon) + decay_rate * master
    )
    return (updated, first_new, second_new)


def fold_kernel(count, widths, extra, scalars, factor_ref, *refs):
    parts = len(widths)
    pieces = [refs[k * parts : (k + 1) * parts] for k in range(count)]
    state = refs[count * parts :]
    factor = factor_ref[0, 0]
    start = 0
    for m in range(count):
        source = scalars[0] ^ m
        for h, width in enumerate(widths):
            gradient = pieces[0][h][:, :width]
            for k in range(1, count):
                gradient = jnp.where(source == k, pieces[k][h][:, :width], gradient)
            put_update(state, start, start + width, gradient, factor)
            start += width
    if extra:
        gradient = pieces[0][0][:, widths[0] :].astype(jnp.float32)
        for k in range(1, count):
            gradient = gradient + pieces[k][0][:, widths[0] :].astype(jnp.float32)
        put_update(state, start, start + extra, gradient, factor)


def put_update(refs, start, stop, gradient, factor):
    master, first, second, updated, first_new, second_new = refs
    state = adam_update(
        master[:, start:stop],
        first[:, start:stop],
        second[:, start:stop],
        gradient.astype(jnp.float32),
        factor,
    )
    updated[:, start:stop] = state[0]
    first_new[:, start:stop] = state[1]
    second_new[:, start:stop] = state[2]


def fold_update(pieces, member, factor, master, first, second, extra):
    count = len(pieces)
    rows, columns = master.shape
    flat = [part for piece in pieces for part in piece]
    widths = [part.shape[1] - extra for part in pieces[0]]
    tile = max(16, rows // 4)
    state_spec = pl.BlockSpec((tile, columns), lambda i, scalars: (i, 0))
    piece_specs = [pl.BlockSpec((tile, p.shape[1]), lambda i, scalars: (i, 0)) for p in flat]
    return pl.pallas_call(
        functools.partial(fold_kernel, count, widths, extra),
        out_shape=[jax.ShapeDtypeStruct(master.shape, jnp.float32)] * 3,
        grid_spec=pltpu.PrefetchScalarGridSpec(
            num_scalar_prefetch=1,
            grid=(rows // tile,),
            in_specs=[pl.BlockSpec(memory_space=pltpu.SMEM)] + piece_specs + [state_spec] * 3,
            out_specs=[state_spec] * 3,
        ),
        name="fold_update",
    )(member.reshape(1), factor.reshape(1, 1), *flat, master, first, second)


def local_step(
    count,
    shard_count,
    hidden_in,
    out_cotangent,
    seg_ids,
    mixer_master,
    mixer_first,
    mixer_second,
    project_master,
    project_first,
    project_second,
    expand_master,
    expand_first,
    expand_second,
    reduce_master,
    reduce_first,
    reduce_second,
    affine_master,
    affine_first,
    affine_second,
):
    member = lax.axis_index("seq")
    shard = lax.axis_index("fsdp")
    shards = shard_count
    counts = (("seq", count), ("fsdp", shards))
    token_count = hidden_in.shape[1]
    group_tokens = token_count * count
    heads = HEADS // count
    width = heads * HEAD
    slab = FF // count
    mixer_low = mixer_master.astype(low)

    def mixer_block(m):
        return jnp.concatenate(
            [lax.dynamic_slice_in_dim(mixer_low, m * width, width, 1), mixer_low[:, D:]], axis=1
        )

    def expand_block(m):
        return lax.dynamic_slice_in_dim(expand_low, m * slab, slab, 1)

    mixer_rows = exchange(mixer_block, member, count)
    project_low = project_master.astype(low)[None]
    mixer_rows, late_expand, late_reduce, seg_ids, hidden_in = lax.optimization_barrier(
        (mixer_rows, expand_master, reduce_master, seg_ids, hidden_in)
    )
    expand_low = late_expand.astype(low)
    hidden = hidden_in[0].astype(jnp.float32)
    segment_rows = seg_ids[0].reshape(count, token_count)
    spans = [0]
    distance = count // 2
    while distance:
        spans = spans + [k ^ distance for k in spans]
        distance //= 2
    owners = [member ^ k for k in spans]
    segments = jnp.concatenate([segment_rows[m] for m in owners])
    places = jnp.concatenate(
        [m * token_count + jnp.arange(token_count, dtype=jnp.int32) for m in owners]
    )

    filler = mixer_rows[0, 0, 0]
    mixer_w = lax.all_gather(mixer_rows, "fsdp", axis=1, tiled=True).reshape(D, width + KV)
    project_w = gather_rows(project_low, shard, shards, filler)
    expand_rows = exchange(expand_block, member, count)
    expand_w = gather_rows(expand_rows, shard, shards, filler)

    ln_one_own = layer_norm(hidden, affine_master[0], affine_master[1]).astype(low)
    ln_one = gather_tokens(ln_one_own, count)
    mixed = product(ln_one, mixer_w).astype(low)
    mixed, reduce_rows = lax.optimization_barrier((mixed, late_reduce.astype(low)))
    reduce_w = lax.all_gather(reduce_rows, "fsdp", axis=0, tiled=True)
    queries = mixed[:, :width].reshape(group_tokens, heads, HEAD)
    key_rows = mixed[:, width : width + HEAD]
    value_rows = mixed[:, width + HEAD :]
    head_out, logsum = attend_forward(queries, key_rows, value_rows, places, segments)
    attended = head_out.reshape(group_tokens, width)

    def project_rows(start, stop):
        return product(attended[start:stop], project_w)

    middle = hidden + scatter_tokens(project_rows, group_tokens, count)
    ln_two = gather_tokens(
        layer_norm(middle, affine_master[2], affine_master[3]).astype(low), count
    )
    cotangent = gather_tokens(out_cotangent[0], count)
    expanded = product(ln_two, expand_w)
    activated = activate(expanded).astype(low)

    reduce_halves = []
    for h in range(2):
        part = column_product(activated, cotangent[:, h * D // 2 : (h + 1) * D // 2])
        reduce_halves.append(scatter_mixed(part[None], shard, shards)[0])
    grad_activated = times_transpose(cotangent, reduce_w)
    _, gelu_pull = jax.vjp(activate, expanded)
    grad_expanded = gelu_pull(grad_activated)[0].astype(low)

    def normed_rows(start, stop):
        return times_transpose(grad_expanded[start:stop], expand_w)

    grad_normed = scatter_tokens(normed_rows, group_tokens, count)
    expand_halves = []
    for h in range(2):
        part = column_product(ln_two, grad_expanded[:, h * slab // 2 : (h + 1) * slab // 2])
        part = scatter_mixed(part.reshape(count, D // count, slab // 2), shard, shards)
        expand_halves.append(trade(lambda m: part[m], member, count))
    expand_pieces = list(zip(*expand_halves))

    _, second_pull = jax.vjp(layer_norm, middle, affine_master[2], affine_master[3])
    grad_inner, gain_two, shift_two = second_pull(grad_normed)
    grad_middle = out_cotangent[0].astype(jnp.float32) + grad_inner
    branch_own = grad_middle.astype(low)
    branch_own, late_activated, late_middle = lax.optimization_barrier(
        (branch_own, activated, middle)
    )
    grad_branch = gather_tokens(branch_own, count)

    def output_rows(start, stop):
        return product(late_activated[start:stop], reduce_w)

    output = late_middle + scatter_tokens(output_rows, group_tokens, count)
    block_output = output.astype(low)[None]
    grad_head = (
        times_transpose(grad_branch, project_w).astype(low).reshape(group_tokens, heads, HEAD)
    )
    project_part = column_product(attended, grad_branch)
    project_grad = scatter_rows(project_part[None], shard, shards)[0]
    query_part, key_value_part = attend_backward(
        queries, key_rows, value_rows, logsum, grad_head, places, segments
    )
    grad_mixed = jnp.concatenate(
        [query_part.reshape(group_tokens, width), key_value_part.astype(low)], axis=1
    )
    mixer_part = column_product(ln_one, grad_mixed)
    mixer_part = scatter_rows(mixer_part.reshape(count, D // count, width + KV), shard, shards)
    mixer_pieces = trade(lambda m: mixer_part[m], member, count)

    def first_rows(start, stop):
        return times_transpose(grad_mixed[start:stop], mixer_w)

    grad_first = scatter_tokens(first_rows, group_tokens, count)
    _, first_pull = jax.vjp(layer_norm, hidden, affine_master[0], affine_master[1])
    grad_hidden, gain_one, shift_one = first_pull(grad_first)
    input_grad = (grad_middle + grad_hidden).astype(low)[None]

    affine_grad = butterfly(jnp.stack([gain_one, shift_one, gain_two, shift_two]), counts)
    expand_squares = [
        jnp.sum(jnp.square(p.astype(jnp.float32))) for ps in [*expand_pieces, reduce_halves] for p in ps
    ]
    mixer_squares = [jnp.sum(jnp.square(p[:, :width])) for p in mixer_pieces]
    shared_grad = sum(p[:, width:] for p in mixer_pieces)
    local_square = (
        sum(mixer_squares)
        + jnp.sum(shared_grad * shared_grad)
        + jnp.sum(project_grad * project_grad)
        + sum(expand_squares)
    )
    square_total = total_over_mesh(local_square, member * shards + shard, counts) + jnp.sum(
        affine_grad * affine_grad
    )
    grad_norm = jnp.sqrt(square_total)
    limit = math.sqrt(float(D * (D + KV) + D * D + 2 * D * FF + 4 * D))
    factor = limit / jnp.maximum(grad_norm, limit)
    mixer_state = fold_update(
        [[p] for p in mixer_pieces], member, factor, mixer_master, mixer_first, mixer_second, KV
    )
    project_state = adam_update(project_master, project_first, project_second, project_grad, factor)
    expand_state = fold_update(
        expand_pieces, member, factor, expand_master, expand_first, expand_second, 0
    )
    reduce_state = fold_update(
        [reduce_halves], member, factor, reduce_master, reduce_first, reduce_second, 0
    )
    affine_state = adam_update(affine_master, affine_first, affine_second, affine_grad, factor)
    return (
        block_output,
        input_grad,
        grad_norm,
        *mixer_state,
        *project_state,
        *expand_state,
        *reduce_state,
        affine_state[0] - affine_master,
        affine_state[1],
        affine_state[2],
    )


def solution(mesh):
    count = mesh.shape["seq"]
    tokens = P("fsdp", "seq", None)
    rows = P(("seq", "fsdp"), None)
    in_specs = (tokens, tokens, P("fsdp", None)) + (rows,) * 12 + (P(),) * 3
    out_specs = (tokens, tokens, P()) + (rows,) * 12 + (P(),) * 3

    def local(*values):
        return local_step(count, mesh.shape["fsdp"], *values)

    return jax.shard_map(local, mesh=mesh, in_specs=in_specs, out_specs=out_specs, check_vma=False)
```

```python
import functools
import math

import jax
import jax.numpy as jnp
from jax import lax
from jax.experimental import pallas as pl
from jax.experimental.pallas import tpu as pltpu
from jax.sharding import PartitionSpec as P


D = 2048
FF = 8192
HEADS = 16
HEAD = 128
STEP = 10
KV = 2 * HEAD

norm_epsilon = 1e-05
adam_epsilon = 1e-08
first_decay = 0.9
second_decay = 0.95
learn_rate = 0.03
decay_rate = 0.1
masked_score = -1e30
low = jnp.bfloat16


def layer_norm(values_in, norm_gain, norm_shift):
    centered = values_in - jnp.mean(values_in, axis=-1, keepdims=True)
    variance = jnp.mean(centered * centered, axis=-1, keepdims=True)
    return centered * lax.rsqrt(variance + norm_epsilon) * norm_gain + norm_shift


def activate(pre_act):
    return jax.nn.gelu(pre_act, approximate=True)


def product(left_side, right_side):
    return jnp.dot(left_side, right_side, preferred_element_type=jnp.float32)


def times_transpose(left_side, right_side):
    return lax.dot_general(
        left_side, right_side, (((1,), (1,)), ((), ())), preferred_element_type=jnp.float32
    )


def column_product(left_side, right_side):
    return lax.dot_general(
        left_side, right_side, (((0,), (0,)), ((), ())), preferred_element_type=jnp.float32
    )


def swap(value, axis, count, distance):
    return lax.ppermute(value, axis, [(i, i ^ distance) for i in range(count)])


def gather_tokens(own, count):
    held = own
    distance = count // 2
    while distance:
        held = jnp.concatenate([held, swap(held, "seq", count, distance)])
        distance //= 2
    return held


def scatter_tokens(make, rows, count):
    held = None
    distance = 1
    while distance < count:
        part = rows // 2
        if held is None:
            leave = make(part, rows).astype(low)
            stay = make(0, part)
        else:
            leave = held[part:].astype(low)
            stay = held[:part]
        held = stay + swap(leave, "seq", count, distance).astype(jnp.float32)
        rows = part
        distance *= 2
    return held


def gather_rows(own, member, count, filler):
    blocks = {0: own}
    distance = count // 2
    while distance:
        for k in sorted(blocks):
            blocks[k ^ distance] = swap(blocks[k], "fsdp", count, distance)
        distance //= 2
    lead, rows, columns = own.shape
    result = jnp.broadcast_to(filler, (lead, count, rows, columns))
    for k in range(count):
        result = lax.dynamic_update_slice_in_dim(result, blocks[k][:, None], member ^ k, 1)
    return result.reshape(lead * count * rows, columns)


def scatter_step(value, member, count, remaining, distance):
    lead, rows, columns = value.shape
    above = 2 ** sum(d > distance for d in remaining)
    pairs = value.reshape(lead, above, 2, rows // (2 * above), columns)
    bit = (member // distance) % 2
    leave = lax.dynamic_index_in_dim(pairs, 1 - bit, 2, keepdims=False)
    come = swap(leave.astype(low), "fsdp", count, distance)
    kept = lax.dynamic_index_in_dim(pairs, bit, 2, keepdims=False) + come.astype(jnp.float32)
    return kept.reshape(lead, rows // 2, columns)


def scatter_rows(value, member, count):
    remaining = [2**k for k in range(count.bit_length() - 1)]
    for distance in list(remaining):
        value = scatter_step(value, member, count, remaining, distance)
        remaining = [d for d in remaining if d != distance]
    return value


def scatter_mixed(value, member, count):
    remaining = [2**k for k in range(count.bit_length() - 1)]
    kept = scatter_step(value, member, count, remaining, 1)
    kept = kept.astype(low)
    groups = [[y + 2 * z for z in range(count // 2)] for y in range(2)]
    return lax.psum_scatter(kept, "fsdp", scatter_dimension=1, tiled=True, axis_index_groups=groups)


def total_over_mesh(value, place, counts):
    spots = jnp.arange(8 * 128, dtype=jnp.int32).reshape(8, 128)
    spread = jnp.where(spots == place, value, 0.0)
    for axis, count in counts:
        come = [swap(spread, axis, count, k) for k in range(1, count)]
        for part in come:
            spread = spread + part
    return jnp.sum(spread)


def butterfly(value, counts):
    for axis, count in counts:
        distance = 1
        while distance < count:
            value = value + swap(value, axis, count, distance)
            distance *= 2
    return value


def trade(block_of, member, count):
    return [block_of(member)] + [
        swap(block_of(member ^ k), "seq", count, k) for k in range(1, count)
    ]


def exchange(block_of, member, count):
    pieces = trade(block_of, member, count)
    result = jnp.broadcast_to(pieces[0], (count,) + pieces[0].shape)
    for k, piece in enumerate(pieces):
        result = lax.dynamic_update_slice_in_dim(result, piece[None], member ^ k, 0)
    return lax.optimization_barrier(result)


def visible(query_place, query_segment, places, segments):
    same_segment = (segments[None, :] == query_segment[:, None]) & (
        places[None, :] <= query_place[:, None]
    )
    prompt_shared = (segments[None, :] == 0) & (query_segment[:, None] != 0)
    return same_segment | prompt_shared


def block_scores(queries, key_rows, places, segments, row_start, block_size):
    query_rows = lax.dynamic_slice_in_dim(queries, row_start, block_size, 0)
    allowed = visible(
        lax.dynamic_slice_in_dim(places, row_start, block_size, 0),
        lax.dynamic_slice_in_dim(segments, row_start, block_size, 0),
        places,
        segments,
    )
    scores = jnp.einsum(
        "qhd,kd->hqk", query_rows, key_rows, preferred_element_type=jnp.float32
    ) * queries.shape[2] ** (-0.5)
    return (query_rows, jnp.where(allowed[None], scores, masked_score))


def attend_forward(queries, key_rows, value_rows, places, segments):
    row_total = queries.shape[0]
    block_size = math.gcd(row_total, 512)

    def one_block(row_start):
        _, scores = block_scores(queries, key_rows, places, segments, row_start, block_size)
        top_score = jnp.max(scores, axis=-1, keepdims=True)
        exp_scores = jnp.exp(scores - top_score)
        exp_total = jnp.sum(exp_scores, axis=-1, keepdims=True)
        probs_low = (exp_scores / exp_total).astype(low)
        mixed_out = jnp.einsum(
            "hqk,kd->qhd", probs_low, value_rows, preferred_element_type=jnp.float32
        )
        return (mixed_out.astype(low), (top_score + jnp.log(exp_total))[:, :, 0])

    block_starts = jnp.arange(0, row_total, block_size, dtype=jnp.int32)
    block_outs, logsum = lax.map(one_block, block_starts)
    return (block_outs.reshape(queries.shape), logsum)


def attend_backward(queries, key_rows, value_rows, logsum, grad_out, places, segments):
    row_total = queries.shape[0]
    block_size = math.gcd(row_total, 512)
    scale = queries.shape[2] ** (-0.5)

    def one_block(carry_in, block_item):
        row_start, block_logsum = block_item
        query_rows, scores = block_scores(
            queries, key_rows, places, segments, row_start, block_size
        )
        probs = jnp.exp(scores - block_logsum[:, :, None])
        grad_rows = lax.dynamic_slice_in_dim(grad_out, row_start, block_size, 0)
        grad_probs = jnp.einsum(
            "qhd,kd->hqk", grad_rows, value_rows, preferred_element_type=jnp.float32
        )
        inner_sum = jnp.sum(probs * grad_probs, axis=-1, keepdims=True)
        grad_scores = (probs * (grad_probs - inner_sum)).astype(low)
        query_grad = (
            jnp.einsum("hqk,kd->qhd", grad_scores, key_rows, preferred_element_type=jnp.float32)
            * scale
        )
        key_grad = (
            carry_in[0]
            + jnp.einsum("hqk,qhd->kd", grad_scores, query_rows, preferred_element_type=jnp.float32)
            * scale
        )
        value_grad = carry_in[1] + jnp.einsum(
            "hqk,qhd->kd", probs.astype(low), grad_rows, preferred_element_type=jnp.float32
        )
        return ((key_grad, value_grad), query_grad.astype(low))

    block_starts = jnp.arange(0, row_total, block_size, dtype=jnp.int32)
    zero_grad = jnp.zeros(key_rows.shape, jnp.float32)
    (key_grad, value_grad), query_grads = lax.scan(
        one_block, (zero_grad, zero_grad), (block_starts, logsum)
    )
    return (query_grads.reshape(queries.shape), jnp.concatenate([key_grad, value_grad], axis=1))


def adam_update(master, first, second, gradient, factor):
    clipped = gradient * factor
    first_new = first_decay * first + (1.0 - first_decay) * clipped
    second_new = second_decay * second + (1.0 - second_decay) * clipped * clipped
    first_hat = first_new / (1.0 - first_decay**STEP)
    second_hat = second_new / (1.0 - second_decay**STEP)
    updated = master - learn_rate * (
        first_hat / (jnp.sqrt(second_hat) + adam_epsilon) + decay_rate * master
    )
    return (updated, first_new, second_new)


def fold_kernel(count, widths, extra, scalars, factor_ref, *refs):
    parts = len(widths)
    pieces = [refs[k * parts : (k + 1) * parts] for k in range(count)]
    state = refs[count * parts :]
    factor = factor_ref[0, 0]
    start = 0
    for m in range(count):
        source = scalars[0] ^ m
        for h, width in enumerate(widths):
            gradient = pieces[0][h][:, :width]
            for k in range(1, count):
                gradient = jnp.where(source == k, pieces[k][h][:, :width], gradient)
            put_update(state, start, start + width, gradient, factor)
            start += width
    if extra:
        gradient = pieces[0][0][:, widths[0] :].astype(jnp.float32)
        for k in range(1, count):
            gradient = gradient + pieces[k][0][:, widths[0] :].astype(jnp.float32)
        put_update(state, start, start + extra, gradient, factor)


def put_update(refs, start, stop, gradient, factor):
    master, first, second, updated, first_new, second_new = refs
    state = adam_update(
        master[:, start:stop],
        first[:, start:stop],
        second[:, start:stop],
        gradient.astype(jnp.float32),
        factor,
    )
    updated[:, start:stop] = state[0]
    first_new[:, start:stop] = state[1]
    second_new[:, start:stop] = state[2]


def fold_update(pieces, member, factor, master, first, second, extra):
    count = len(pieces)
    rows, columns = master.shape
    flat = [part for piece in pieces for part in piece]
    widths = [part.shape[1] - extra for part in pieces[0]]
    tile = max(16, rows // 4)
    state_spec = pl.BlockSpec((tile, columns), lambda i, scalars: (i, 0))
    piece_specs = [pl.BlockSpec((tile, p.shape[1]), lambda i, scalars: (i, 0)) for p in flat]
    return pl.pallas_call(
        functools.partial(fold_kernel, count, widths, extra),
        out_shape=[jax.ShapeDtypeStruct(master.shape, jnp.float32)] * 3,
        grid_spec=pltpu.PrefetchScalarGridSpec(
            num_scalar_prefetch=1,
            grid=(rows // tile,),
            in_specs=[pl.BlockSpec(memory_space=pltpu.SMEM)] + piece_specs + [state_spec] * 3,
            out_specs=[state_spec] * 3,
        ),
        name="fold_update",
    )(member.reshape(1), factor.reshape(1, 1), *flat, master, first, second)


def local_step(
    count,
    shard_count,
    hidden_in,
    out_cotangent,
    seg_ids,
    mixer_master,
    mixer_first,
    mixer_second,
    project_master,
    project_first,
    project_second,
    expand_master,
    expand_first,
    expand_second,
    reduce_master,
    reduce_first,
    reduce_second,
    affine_master,
    affine_first,
    affine_second,
):
    member = lax.axis_index("seq")
    shard = lax.axis_index("fsdp")
    shards = shard_count
    counts = (("seq", count), ("fsdp", shards))
    token_count = hidden_in.shape[1]
    group_tokens = token_count * count
    heads = HEADS // count
    width = heads * HEAD
    slab = FF // count
    mixer_low = mixer_master.astype(low)

    def mixer_block(m):
        return jnp.concatenate(
            [lax.dynamic_slice_in_dim(mixer_low, m * width, width, 1), mixer_low[:, D:]], axis=1
        )

    def expand_block(m):
        return lax.dynamic_slice_in_dim(expand_low, m * slab, slab, 1)

    mixer_rows = exchange(mixer_block, member, count)
    project_low = project_master.astype(low)[None]
    mixer_rows, late_expand, late_reduce, seg_ids, hidden_in = lax.optimization_barrier(
        (mixer_rows, expand_master, reduce_master, seg_ids, hidden_in)
    )
    expand_low = late_expand.astype(low)
    hidden = hidden_in[0].astype(jnp.float32)
    segment_rows = seg_ids[0].reshape(count, token_count)
    spans = [0]
    distance = count // 2
    while distance:
        spans = spans + [k ^ distance for k in spans]
        distance //= 2
    owners = [member ^ k for k in spans]
    segments = jnp.concatenate([segment_rows[m] for m in owners])
    places = jnp.concatenate(
        [m * token_count + jnp.arange(token_count, dtype=jnp.int32) for m in owners]
    )

    filler = mixer_rows[0, 0, 0]
    mixer_w = lax.all_gather(mixer_rows, "fsdp", axis=1, tiled=True).reshape(D, width + KV)
    project_w = gather_rows(project_low, shard, shards, filler)
    expand_rows = exchange(expand_block, member, count)
    expand_w = gather_rows(expand_rows, shard, shards, filler)

    ln_one_own = layer_norm(hidden, affine_master[0], affine_master[1]).astype(low)
    ln_one = gather_tokens(ln_one_own, count)
    mixed = product(ln_one, mixer_w).astype(low)
    queries = mixed[:, :width].reshape(group_tokens, heads, HEAD)
    key_rows = mixed[:, width : width + HEAD]
    value_rows = mixed[:, width + HEAD :]
    head_out, logsum = attend_forward(queries, key_rows, value_rows, places, segments)
    head_out, reduce_rows = lax.optimization_barrier((head_out, late_reduce.astype(low)))
    reduce_w = lax.all_gather(reduce_rows, "fsdp", axis=0, tiled=True)
    attended = head_out.reshape(group_tokens, width)

    def project_rows(start, stop):
        return product(attended[start:stop], project_w)

    middle = hidden + scatter_tokens(project_rows, group_tokens, count)
    ln_two = gather_tokens(
        layer_norm(middle, affine_master[2], affine_master[3]).astype(low), count
    )
    cotangent = gather_tokens(out_cotangent[0], count)
    expanded = product(ln_two, expand_w)
    activated = activate(expanded).astype(low)

    squares = []
    reduce_halves = []
    for h in range(2):
        part = column_product(activated, cotangent[:, h * D // 2 : (h + 1) * D // 2])
        reduce_halves.append(scatter_mixed(part[None], shard, shards)[0])
        squares.append(jnp.sum(jnp.square(reduce_halves[h].astype(jnp.float32))))
    grad_activated = times_transpose(cotangent, reduce_w)
    _, gelu_pull = jax.vjp(activate, expanded)
    grad_expanded = gelu_pull(grad_activated)[0].astype(low)

    def normed_rows(start, stop):
        return times_transpose(grad_expanded[start:stop], expand_w)

    grad_normed = scatter_tokens(normed_rows, group_tokens, count)
    expand_halves = []
    for h in range(2):
        part = column_product(ln_two, grad_expanded[:, h * slab // 2 : (h + 1) * slab // 2])
        part = scatter_mixed(part.reshape(count, D // count, slab // 2), shard, shards)
        squares.append(jnp.sum(jnp.square(part.astype(jnp.float32))))
        expand_halves.append(trade(lambda m: part[m], member, count))
    expand_pieces = list(zip(*expand_halves))

    _, second_pull = jax.vjp(layer_norm, middle, affine_master[2], affine_master[3])
    grad_inner, gain_two, shift_two = second_pull(grad_normed)
    grad_middle = out_cotangent[0].astype(jnp.float32) + grad_inner
    branch_own = grad_middle.astype(low)
    branch_own, late_activated, late_middle = lax.optimization_barrier(
        (branch_own, activated, middle)
    )
    grad_branch = gather_tokens(branch_own, count)

    def output_rows(start, stop):
        return product(late_activated[start:stop], reduce_w)

    output = late_middle + scatter_tokens(output_rows, group_tokens, count)
    block_output = output.astype(low)[None]
    grad_head = (
        times_transpose(grad_branch, project_w).astype(low).reshape(group_tokens, heads, HEAD)
    )
    project_part = column_product(attended, grad_branch)
    project_grad = scatter_rows(project_part[None], shard, shards)[0]
    query_part, key_value_part = attend_backward(
        queries, key_rows, value_rows, logsum, grad_head, places, segments
    )
    grad_mixed = jnp.concatenate(
        [query_part.reshape(group_tokens, width), key_value_part.astype(low)], axis=1
    )
    mixer_part = column_product(ln_one, grad_mixed)
    mixer_part = scatter_rows(mixer_part.reshape(count, D // count, width + KV), shard, shards)
    squares.append(jnp.sum(jnp.square(mixer_part[:, :, :width])))
    mixer_pieces = trade(lambda m: mixer_part[m], member, count)

    def first_rows(start, stop):
        return times_transpose(grad_mixed[start:stop], mixer_w)

    grad_first = scatter_tokens(first_rows, group_tokens, count)
    _, first_pull = jax.vjp(layer_norm, hidden, affine_master[0], affine_master[1])
    grad_hidden, gain_one, shift_one = first_pull(grad_first)
    input_grad = (grad_middle + grad_hidden).astype(low)[None]

    affine_grad = butterfly(jnp.stack([gain_one, shift_one, gain_two, shift_two]), counts)
    shared_grad = sum(p[:, width:] for p in mixer_pieces)
    squares.append(jnp.sum(shared_grad * shared_grad))
    squares.append(jnp.sum(project_grad * project_grad))
    local_square = sum(squares)
    square_total = total_over_mesh(local_square, member * shards + shard, counts) + jnp.sum(
        affine_grad * affine_grad
    )
    grad_norm = jnp.sqrt(square_total)
    limit = math.sqrt(float(D * (D + KV) + D * D + 2 * D * FF + 4 * D))
    factor = limit / jnp.maximum(grad_norm, limit)
    mixer_state = fold_update(
        [[p] for p in mixer_pieces], member, factor, mixer_master, mixer_first, mixer_second, KV
    )
    project_state = adam_update(project_master, project_first, project_second, project_grad, factor)
    expand_state = fold_update(
        expand_pieces, member, factor, expand_master, expand_first, expand_second, 0
    )
    reduce_state = fold_update(
        [reduce_halves], member, factor, reduce_master, reduce_first, reduce_second, 0
    )
    affine_state = adam_update(affine_master, affine_first, affine_second, affine_grad, factor)
    return (
        block_output,
        input_grad,
        grad_norm,
        *mixer_state,
        *project_state,
        *expand_state,
        *reduce_state,
        affine_state[0] - affine_master,
        affine_state[1],
        affine_state[2],
    )


def solution(mesh):
    count = mesh.shape["seq"]
    tokens = P("fsdp", "seq", None)
    rows = P(("seq", "fsdp"), None)
    in_specs = (tokens, tokens, P("fsdp", None)) + (rows,) * 12 + (P(),) * 3
    out_specs = (tokens, tokens, P()) + (rows,) * 12 + (P(),) * 3

    def local(*values):
        return local_step(count, mesh.shape["fsdp"], *values)

    return jax.shard_map(local, mesh=mesh, in_specs=in_specs, out_specs=out_specs, check_vma=False)
```
